32 devices in a mesh: dp: 8 (over y, x, core), seq: 4 (over z).
Axes of the slice: x: 2, y: 2, z: 4, core: 2. Of those that a mesh axis runs over, the one named last changes fastest.
Arguments:
- block_input: bfloat16 [16, 580, 1024], P('dp', 'seq'), may hold values from -6 to 6
- live_mask: int32 [16, 580], P('dp', 'seq'), may hold values from 0 to 1, as said below
- cotangent: bfloat16 [16, 580, 1024], P('dp', 'seq'), may hold values from -6 to 6
- joint_weight: float32 [2, 1024, 3072], P(None, ('dp', 'seq')), may hold values from -0.1875 to 0.1875
- output_weight: float32 [2, 1024, 1024], P(None, ('dp', 'seq')), may hold values from -0.75 to 0.75
- expand_weight: float32 [2, 1024, 4096], P(None, ('dp', 'seq')), may hold values from -0.1875 to 0.1875
- reduce_weight: float32 [2, 4096, 1024], P(None, ('dp', 'seq')), may hold values from -0.09375 to 0.09375
- norm_gains: float32 [2, 2, 1024], P(None, None, ('dp', 'seq')), may hold values from 0.5 to 1.5
- all_biases: float32 [2, 10, 1024], P(None, None, ('dp', 'seq')), may hold values from -2 to 2
- momentum_joint: float32 [2, 1024, 3072], P(None, ('dp', 'seq')), may hold values from -28 to 28
- momentum_output: float32 [2, 1024, 1024], P(None, ('dp', 'seq')), may hold values from -28 to 28
- momentum_expand: float32 [2, 1024, 4096], P(None, ('dp', 'seq')), may hold values from -28 to 28
- momentum_reduce: float32 [2, 4096, 1024], P(None, ('dp', 'seq')), may hold values from -28 to 28
- momentum_gains: float32 [2, 2, 1024], P(None, None, ('dp', 'seq')), may hold values from -28 to 28
- momentum_biases: float32 [2, 10, 1024], P(None, None, ('dp', 'seq')), may hold values from -28 to 28
- variance_joint: float32 [2, 1024, 3072], P(None, ('dp', 'seq')), may hold values from 1.856 to 18.56
- variance_output: float32 [2, 1024, 1024], P(None, ('dp', 'seq')), may hold values from 1.856 to 18.56
- variance_expand: float32 [2, 1024, 4096], P(None, ('dp', 'seq')), may hold values from 1.856 to 18.56
- variance_reduce: float32 [2, 4096, 1024], P(None, ('dp', 'seq')), may hold values from 1.856 to 18.56
- variance_gains: float32 [2, 2, 1024], P(None, None, ('dp', 'seq')), may hold values from 1.856 to 18.56
- variance_biases: float32 [2, 10, 1024], P(None, None, ('dp', 'seq')), may hold values from 1.856 to 18.56
Outputs:
- block_output: float32 [16, 580, 1024], P('dp', 'seq')
- input_grad: float32 [16, 580, 1024], P('dp', 'seq')
- gradient_joint: float32 [2, 1024, 3072], P(None, ('dp', 'seq'))
- gradient_output: float32 [2, 1024, 1024], P(None, ('dp', 'seq'))
- gradient_expand: float32 [2, 1024, 4096], P(None, ('dp', 'seq'))
- gradient_reduce: float32 [2, 4096, 1024], P(None, ('dp', 'seq'))
- gradient_gains: float32 [2, 2, 1024], P(None, None, ('dp', 'seq'))
- gradient_biases: float32 [2, 10, 1024], P(None, None, ('dp', 'seq'))
- momentum_joint_next: float32 [2, 1024, 3072], P(None, ('dp', 'seq'))
- momentum_output_next: float32 [2, 1024, 1024], P(None, ('dp', 'seq'))
- momentum_expand_next: float32 [2, 1024, 4096], P(None, ('dp', 'seq'))
- momentum_reduce_next: float32 [2, 4096, 1024], P(None, ('dp', 'seq'))
- momentum_gains_next: float32 [2, 2, 1024], P(None, None, ('dp', 'seq'))
- momentum_biases_next: float32 [2, 10, 1024], P(None, None, ('dp', 'seq'))
- variance_joint_next: float32 [2, 1024, 3072], P(None, ('dp', 'seq'))
- variance_output_next: float32 [2, 1024, 1024], P(None, ('dp', 'seq'))
- variance_expand_next: float32 [2, 1024, 4096], P(None, ('dp', 'seq'))
- variance_reduce_next: float32 [2, 4096, 1024], P(None, ('dp', 'seq'))
- variance_gains_next: float32 [2, 2, 1024], P(None, None, ('dp', 'seq'))
- variance_biases_next: float32 [2, 10, 1024], P(None, None, ('dp', 'seq'))
- update_joint: float32 [2, 1024, 3072], P(None, ('dp', 'seq'))
- update_output: float32 [2, 1024, 1024], P(None, ('dp', 'seq'))
- update_expand: float32 [2, 1024, 4096], P(None, ('dp', 'seq'))
- update_reduce: float32 [2, 4096, 1024], P(None, ('dp', 'seq'))
- update_gains: float32 [2, 2, 1024], P(None, None, ('dp', 'seq'))
- update_biases: float32 [2, 10, 1024], P(None, None, ('dp', 'seq'))
The draws below stay inside these ranges and needn't reach their ends.
Inputs may be any that keep to these rules, and one draw needn't show every extreme that they name: `live_mask`: in each image the real tokens come first and the last 0 to 3 positions are padding; some image has 3 padded positions and some has none.
All inputs are finite; a program needn't handle non-finite values.
Results may differ from the reference program's by a relative error of at most 0.014.
Values may be sent and summed in bfloat16 or wider, within the bound.
No kernel may reach another device: no remote copies, remote signals or barrier semaphores. Data moves between devices by JAX's collectives and lax.ppermute only.
A program may use at most 256 MiB of HBM per device.

```python
import math
import jax
import jax.numpy as jnp
from jax import lax

D = 1024
H = 16
HD = 64
FF = 4096
SEQ = 580
L = 2
STEP = 10
IMAGES = 16
BV = 10


def draw_live_mask(key, part):
    pads = jax.random.randint(jax.random.fold_in(key, 17), (IMAGES,), 0, 4)
    pads = pads.at[0].set(3).at[IMAGES - 1].set(0)
    positions = jnp.arange(SEQ, dtype=jnp.int32)
    return (positions[None, :] < (SEQ - pads)[:, None]).astype(jnp.int32)


def strengthened(drawn, stream_key, source, target, parts, factor):
    def block_of(dim):
        return (jnp.arange(drawn.shape[dim]) // (drawn.shape[dim] // parts)).reshape((-1,) + (1,) * (drawn.ndim - 1 - dim))

    first = jax.random.permutation(stream_key, parts)[block_of(target)]
    far = (block_of(target) + parts // 2) % parts
    return jnp.where((block_of(source) == first) | (block_of(source) == far), factor * drawn, drawn)


def level_of(stream_key, shape, cuts, smallest, top_value):
    level = 1.0
    for axis_at, blocks in cuts:
        steps = jax.random.uniform(jax.random.fold_in(jax.random.fold_in(stream_key, 6), axis_at), (blocks,), jnp.float32, smallest / len(cuts), top_value / len(cuts))
        level = level * jnp.repeat(jnp.exp(steps), shape[axis_at] // blocks).reshape((-1,) + (1,) * (len(shape) - 1 - axis_at))
    return level


def gaussian(rng, extent, scale, bound, split=(), kind=jnp.bfloat16):
    values = jax.random.normal(rng, extent, jnp.float32) * scale
    if len(split) > 0:
        values = level_of(rng, extent, split, -0.22, 0.18) * values
    return jnp.clip(values, min=-bound, max=bound).astype(kind)


def bell_draw_with(own_key, dims, width, reach, split, heavy, kind=jnp.bfloat16):
    entries = width * jax.random.normal(own_key, dims, jnp.float32)
    if split:
        entries = entries * level_of(own_key, dims, split, -0.22, 0.18)
    return jnp.clip(strengthened(entries, jax.random.fold_in(own_key, 3), *heavy), -reach, reach).astype(kind)


def setup_inputs(seed: int = 0) -> dict:
    key_of = jax.random.split(jax.random.key(seed), 22)
    return {
        "block_input": bell_draw_with(key_of[0], (IMAGES, SEQ, D), 1.0, 6.0, ((0, 8), (1, 4)), (0, 2, 8, 2.0)),
        "live_mask": draw_live_mask(jax.random.fold_in(key_of[21], 71), 0),
        "cotangent": gaussian(key_of[2], (IMAGES, SEQ, D), 1.0, 6.0, ((0, 8), (1, 4))),
        "joint_weight": gaussian(key_of[3], (L, D, 3 * D), D ** -0.5, 0.1875, ((1, 32),), jnp.float32),
        "output_weight": gaussian(key_of[4], (L, D, D), (D // 16) ** -0.5, 0.75, ((1, 32),), jnp.float32),
        "expand_weight": gaussian(key_of[5], (L, D, FF), D ** -0.5, 0.1875, ((1, 32),), jnp.float32),
        "reduce_weight": gaussian(key_of[6], (L, FF, D), FF ** -0.5, 0.09375, ((1, 32),), jnp.float32),
        "norm_gains": jnp.clip(1.0 + 0.1 * jax.random.normal(key_of[7], (L, 2, D), jnp.float32), 0.5, 1.5),
        "all_biases": gaussian(key_of[8], (L, BV, D), 0.3, 2.0, ((2, 32),), jnp.float32),
        "momentum_joint": gaussian(key_of[9], (L, D, 3 * D), (0.05 * (IMAGES * SEQ) ** 0.5), 28.0, ((1, 32),), jnp.float32),
        "momentum_output": gaussian(key_of[10], (L, D, D), (0.05 * (IMAGES * SEQ) ** 0.5), 28.0, ((1, 32),), jnp.float32),
        "momentum_expand": gaussian(key_of[11], (L, D, FF), (0.05 * (IMAGES * SEQ) ** 0.5), 28.0, ((1, 32),), jnp.float32),
        "momentum_reduce": gaussian(key_of[12], (L, FF, D), (0.05 * (IMAGES * SEQ) ** 0.5), 28.0, ((1, 32),), jnp.float32),
        "momentum_gains": gaussian(key_of[13], (L, 2, D), (0.05 * (IMAGES * SEQ) ** 0.5), 28.0, ((2, 32),), jnp.float32),
        "momentum_biases": gaussian(key_of[14], (L, BV, D), (0.05 * (IMAGES * SEQ) ** 0.5), 28.0, ((2, 32),), jnp.float32),
        "variance_joint": jnp.clip(jnp.exp(math.log(18.56) - 2.3025851 * jax.random.uniform(key_of[15], (L, D, 3 * D), jnp.float32) ** level_of(key_of[15], (L, D, 3 * D), ((1, 32),), -0.2, 0.2)), 1.856, 18.56),
        "variance_output": jnp.clip(jnp.exp(math.log(18.56) - 2.3025851 * jax.random.uniform(key_of[16], (L, D, D), jnp.float32) ** level_of(key_of[16], (L, D, D), ((1, 32),), -0.2, 0.2)), 1.856, 18.56),
        "variance_expand": jnp.clip(jnp.exp(math.log(18.56) - 2.3025851 * jax.random.uniform(key_of[17], (L, D, FF), jnp.float32) ** level_of(key_of[17], (L, D, FF), ((1, 32),), -0.2, 0.2)), 1.856, 18.56),
        "variance_reduce": jnp.clip(jnp.exp(math.log(18.56) - 2.3025851 * jax.random.uniform(key_of[18], (L, FF, D), jnp.float32) ** level_of(key_of[18], (L, FF, D), ((1, 32),), -0.2, 0.2)), 1.856, 18.56),
        "variance_gains": jnp.clip(jnp.exp(math.log(18.56) - 2.3025851 * jax.random.uniform(key_of[19], (L, 2, D), jnp.float32) ** level_of(key_of[19], (L, 2, D), ((2, 32),), -0.2, 0.2)), 1.856, 18.56),
        "variance_biases": jnp.clip(jnp.exp(math.log(18.56) - 2.3025851 * jax.random.uniform(key_of[20], (L, BV, D), jnp.float32) ** level_of(key_of[20], (L, BV, D), ((2, 32),), -0.2, 0.2)), 1.856, 18.56),
    }


@jax.custom_vjp
def low(v):
    return lax.optimization_barrier(v.astype(jnp.bfloat16)).astype(jnp.float32)

@jax.custom_vjp
def low_back(v):
    return v

def low_keep(v):
    return (low(v), None)

def low_pass(kept, grad):
    return (grad,)

def back_keep(v):
    return (v, None)

def back_low(kept, grad):
    return (low(grad),)
low.defvjp(low_keep, low_pass)
low_back.defvjp(back_keep, back_low)
highest = lax.Precision.HIGHEST
eps_norm = 1e-06
beta_one = 0.9
beta_two = 0.999
adam_eps = 1e-08
rate = 0.02
decay = 0.05
neg_big = -1e+30

def matmul(left, right):
    return jnp.dot(left, right, precision=highest)

def normalize(stream, gain, shift):
    average = lax.optimization_barrier(jnp.mean(stream, axis=-1, keepdims=True))
    centred = stream - average
    spread = lax.optimization_barrier(jnp.mean(centred * centred, axis=-1, keepdims=True))
    return centred * lax.rsqrt(spread + eps_norm) * gain + shift

def layer_forward(stream, live, joint_w, output_w, expand_w, reduce_w, gain_w, shift_w):
    image_count = stream.shape[0]
    flat = stream.reshape(-1, D)
    normed_first = low(normalize(flat, gain_w[0], shift_w[0]))
    joint_bias = jnp.concatenate([shift_w[1], jnp.zeros((D,), jnp.float32), shift_w[2]])
    joint = low(low_back(matmul(normed_first, joint_w) + joint_bias))
    joint = joint.reshape(image_count, SEQ, 3, H, HD)
    scores = jnp.einsum('bqhd,bkhd->bhqk', joint[:, :, 0], joint[:, :, 1], precision=highest) * HD ** (-0.5)
    scores = low_back(jnp.where(live[:, None, None, :] > 0, scores, neg_big))
    attn_probs = jax.nn.softmax(scores, axis=-1)
    mixed = jnp.einsum('bhqk,bkhd->bqhd', low(attn_probs), joint[:, :, 2], precision=highest)
    mixed = low(low_back(mixed.reshape(-1, D)))
    middle = flat + low_back(matmul(mixed, output_w) + shift_w[3])
    normed_second = low(normalize(middle, gain_w[1], shift_w[4]))
    expanded = low_back(matmul(normed_second, expand_w) + shift_w[5:5 + FF // D].reshape(-1))
    activated = low(jax.nn.gelu(expanded, approximate=False))
    result = middle + low_back(matmul(activated, reduce_w) + shift_w[5 + FF // D])
    return result.reshape(stream.shape)

def block_forward(stream, live, params):
    for layer_index in range(L):
        joint_w, output_w, expand_w, reduce_w, gain_w, shift_w = tuple((low(param[layer_index]) for param in params))
        stream = layer_forward(stream, live, joint_w, output_w, expand_w, reduce_w, gain_w, shift_w)
    return stream * live[:, :, None].astype(jnp.float32)

def adamw_update(weight, gradient, first, second, shrink):
    first_new = beta_one * first + (1.0 - beta_one) * gradient
    second_new = beta_two * second + (1.0 - beta_two) * gradient * gradient
    first_hat = first_new / (1.0 - beta_one ** STEP)
    second_hat = second_new / (1.0 - beta_two ** STEP)
    delta = -rate * (first_hat / (jnp.sqrt(second_hat) + adam_eps) + shrink * weight)
    return (first_new, second_new, delta)

def reference(block_input, live_mask, cotangent, joint_weight, output_weight, expand_weight, reduce_weight, norm_gains, all_biases, momentum_joint, momentum_output, momentum_expand, momentum_reduce, momentum_gains, momentum_biases, variance_joint, variance_output, variance_expand, variance_reduce, variance_gains, variance_biases):
    params = (joint_weight, output_weight, expand_weight, reduce_weight, norm_gains, all_biases)
    momenta = (momentum_joint, momentum_output, momentum_expand, momentum_reduce, momentum_gains, momentum_biases)
    variances = (variance_joint, variance_output, variance_expand, variance_reduce, variance_gains, variance_biases)
    group = math.gcd(IMAGES, 4)
    groups = IMAGES // group
    inputs = block_input.astype(jnp.float32).reshape(groups, group, SEQ, D)
    lives = live_mask.reshape(groups, group, SEQ)
    cotans = cotangent.astype(jnp.float32).reshape(groups, group, SEQ, D)

    def one_group(totals, pieces):
        stream, live, cotan = pieces

        def local(inner_stream, inner_params):
            return block_forward(inner_stream, live, inner_params)
        output, pull = jax.vjp(local, stream, params)
        grad_stream, grad_params = pull(cotan)
        totals = jax.tree.map(jnp.add, totals, grad_params)
        return (totals, (output, grad_stream))
    zeros = jax.tree.map(jnp.zeros_like, params)
    totals, (outputs, grad_inputs) = lax.scan(one_group, zeros, (inputs, lives, cotans))
    block_output = outputs.reshape(IMAGES, SEQ, D)
    input_grad = grad_inputs.reshape(IMAGES, SEQ, D)
    firsts = []
    seconds = []
    deltas = []
    for position in range(6):
        shrink = decay if position < 4 else 0.0
        first_new, second_new, delta = adamw_update(params[position], totals[position], momenta[position], variances[position], shrink)
        firsts.append(first_new)
        seconds.append(second_new)
        deltas.append(delta)
    return tuple([block_output, input_grad] + list(totals) + firsts + seconds + deltas)
```

```python
import jax
import jax.numpy as jnp
from jax import lax
from jax.sharding import Mesh, PartitionSpec as P

HD = 64
STEP = 10


eps_norm = 1e-06
beta_one = 0.9
beta_two = 0.999
adam_eps = 1e-08
rate = 0.02
decay = 0.05
neg_big = -1e30


low = jnp.bfloat16
wide = jnp.float32


def my_bit(name, bit):
    return (lax.axis_index(name) >> bit) & 1


def swap(block, name, mask):
    size = lax.axis_size(name)
    return lax.ppermute(block, name, [(i, i ^ mask) for i in range(size)])


def join(mine, theirs, name, bit, axis):
    first = my_bit(name, bit) == 0
    return jnp.stack(
        [jnp.where(first, mine, theirs), jnp.where(first, theirs, mine)], axis=axis
    )


def double(block, name, bit, axis):
    return join(block, swap(block, name, 1 << bit), name, bit, axis)


def pick(block, which, axis):
    return lax.dynamic_index_in_dim(block, which, axis, keepdims=False)


def halve(block, name, bit, axis, kind=low):
    bit_here = my_bit(name, bit)
    sent = pick(block, 1 - bit_here, axis).astype(kind)
    kept = pick(block, bit_here, axis).astype(wide)
    return kept + swap(sent, name, 1 << bit).astype(wide)


def bits_of(name):
    return lax.axis_size(name).bit_length() - 1


def gather_block(shard, lead):
    block = shard
    spread = 0
    for name in ("mid", "line"):
        pass
    for bit in reversed(range(bits_of("line"))):
        block = double(block, "line", bit, lead + spread)
        spread += 1
    for bit in range(bits_of("mid")):
        block = double(block, "mid", bit, lead)
    cols = block.shape[-1]
    count = bits_of("top")
    one, two = block[..., : cols // 2], block[..., cols // 2 :]
    for bit in range(count):
        one = double(one, "top", bit, 0)
    for place, bit in enumerate(reversed(range(count))):
        two = double(two, "top", bit, place)
    return jnp.concatenate(
        [one.reshape(-1, cols // 2), two.reshape(-1, cols // 2)], axis=1
    )


def scatter_block(terms, lead, rows):
    cols = terms.shape[-1]
    count = bits_of("top")
    shape = (
        (2,) * count
        + (2,) * lead
        + (2,) * bits_of("mid")
        + (2,) * bits_of("line")
        + (rows, cols // 2)
    )
    one = terms[:, : cols // 2].reshape(shape)
    two = terms[:, cols // 2 :].reshape(shape)
    for bit in reversed(range(count)):
        one = halve(one, "top", bit, 0)
    for bit in range(count):
        two = halve(two, "top", bit, count - 1 - bit)
    block = jnp.concatenate([one, two], axis=-1)
    for bit in reversed(range(bits_of("mid"))):
        block = halve(block, "mid", bit, lead)
    for bit in range(bits_of("line")):
        block = halve(block, "line", bit, lead + bits_of("line") - 1 - bit)
    return block


def joint_columns(rows_block, tops):
    rows, cols = rows_block.shape
    block = cols // (3 * tops * 2)
    view = rows_block.reshape(rows, 3, 2, tops // 2, 2, block)
    return view.transpose(4, 0, 2, 1, 3, 5).reshape(2, rows, cols // 2)


def joint_columns_back(paired, tops):
    pair, rows, half = paired.shape
    block = half // (3 * tops)
    view = paired.reshape(2, rows, 2, 3, tops // 2, block)
    return view.transpose(1, 3, 2, 4, 0, 5).reshape(rows, 2 * half)


def expand_columns(rows_block, tops):
    rows, cols = rows_block.shape
    block = cols // (tops * 2)
    return rows_block.reshape(rows, tops, 2, block).transpose(2, 0, 1, 3).reshape(2, rows, cols // 2)


def expand_columns_back(paired, tops):
    pair, rows, half = paired.shape
    return paired.reshape(2, rows, tops, half // tops).transpose(1, 2, 0, 3).reshape(rows, 2 * half)


def trade(paired):
    here = lax.axis_index("pair")
    mine = pick(paired, here, 0)
    theirs = swap(pick(paired, 1 - here, 0), "pair", 1)
    return join(mine, theirs, "pair", 0, 0)


def order_line(parts):
    here = lax.axis_index("line")
    count = len(parts)
    step = 1
    while step < count:
        odd = (here & step) != 0
        parts = [jnp.where(odd, parts[i ^ step], parts[i]) for i in range(count)]
        step *= 2
    return jnp.stack(parts)


def trade_line(blocks):
    here = lax.axis_index("line")
    count = lax.axis_size("line")
    parts = [pick(blocks, here, 0)]
    for d in range(1, count):
        parts.append(swap(pick(blocks, here ^ d, 0), "line", d))
    return order_line(parts)


def to_images(tokens):
    count, length, width = tokens.shape
    here = lax.axis_index("pair")
    view = tokens.reshape(count, length, 2, width // 2)
    mine = pick(view, here, 2)
    theirs = swap(pick(view, 1 - here, 2), "pair", 1)
    images = join(mine, theirs, "pair", 0, 0).reshape(2 * count, length, width // 2)
    whole = trade_line(images).reshape(-1, width // 2)
    other = swap(whole, "pair", 1)
    first = here == 0
    return jnp.concatenate(
        [jnp.where(first, whole, other), jnp.where(first, other, whole)], axis=1
    )


def from_images(rows, count, length):
    width = rows.shape[1]
    here = lax.axis_index("pair")
    lines = lax.axis_size("line")
    half = pick(rows.reshape(lines, length, 2, width // 2), here, 2)
    images = trade_line(half).reshape(2, count, length, width // 2)
    mine = pick(images, here, 0)
    theirs = swap(pick(images, 1 - here, 0), "pair", 1)
    first = here == 0
    return jnp.concatenate(
        [jnp.where(first, mine, theirs), jnp.where(first, theirs, mine)], axis=-1
    )


def mask_of_image(live):
    block = double(live, "pair", 0, 0).reshape(-1, live.shape[1])
    spread = 1
    for bit in reversed(range(bits_of("line"))):
        block = double(block, "line", bit, spread)
        spread += 1
    return pick(block.reshape(block.shape[0], -1), lax.axis_index("line"), 0)


def normalize(stream, gain, shift):
    average = jnp.mean(stream, axis=-1, keepdims=True)
    centred = stream - average
    spread = jnp.mean(centred * centred, axis=-1, keepdims=True)
    return centred * lax.rsqrt(spread + eps_norm) * gain + shift


def gelu_exact(values):
    return jax.nn.gelu(values, approximate=False)


def dot(left, right):
    return jnp.dot(left, right, preferred_element_type=wide)


def pair_sum(partial):
    return partial + swap(partial.astype(low), "pair", 1).astype(wide)


def split_heads(joint):
    rows = joint.shape[0]
    view = joint.reshape(rows, 2, 3, -1, HD)
    return tuple(view[:, :, k].reshape(rows, -1, HD) for k in range(3))


def join_heads(parts):
    rows = parts[0].shape[0]
    views = [part.reshape(rows, 2, 1, -1) for part in parts]
    return jnp.concatenate(views, axis=2).reshape(rows, -1)


def scores_of(queries, keys, live):
    scores = jnp.einsum("qhd,khd->hqk", queries, keys, preferred_element_type=wide) * HD ** (-0.5)
    return jnp.where(live[None, None, :] > 0, scores, neg_big)


def attend(queries, keys, values, live):
    scores = scores_of(queries, keys, live)
    top = jnp.max(scores, axis=-1, keepdims=True)
    log_total = top + jnp.log(jnp.sum(jnp.exp(scores - top), axis=-1, keepdims=True))
    probs = jnp.exp(scores - log_total).astype(low)
    mixed = jnp.einsum("hqk,khd->qhd", probs, values, preferred_element_type=wide)
    return mixed.astype(low), log_total


def attend_back(queries, keys, values, live, log_total, grad_mixed):
    probs = jnp.exp(scores_of(queries, keys, live) - log_total)
    grad_probs = jnp.einsum("qhd,khd->hqk", grad_mixed, values, preferred_element_type=wide)
    grad_values = jnp.einsum("hqk,qhd->khd", probs.astype(low), grad_mixed, preferred_element_type=wide)
    inner = jnp.sum(probs * grad_probs, axis=-1, keepdims=True)
    grad_scores = (probs * (grad_probs - inner)).astype(low)
    scale = HD ** (-0.5)
    grad_queries = jnp.einsum("hqk,khd->qhd", grad_scores, keys, preferred_element_type=wide) * scale
    grad_keys = jnp.einsum("hqk,qhd->khd", grad_scores, queries, preferred_element_type=wide) * scale
    return grad_queries, grad_keys, grad_values


def forward_layer(stream, live, weights, vectors):
    joint_w, output_w, expand_w, reduce_w = weights
    gains, shifts, joint_bias, expand_bias = vectors
    normed_first = normalize(stream, gains[0], shifts[0]).astype(low)
    joint = (dot(normed_first, joint_w) + joint_bias).astype(low)
    queries, keys, values = split_heads(joint)
    mixed, log_total = attend(queries, keys, values, live)
    mixed = mixed.reshape(stream.shape[0], -1)
    middle = stream + pair_sum(dot(mixed, output_w)) + shifts[3]
    normed_second = normalize(middle, gains[1], shifts[4]).astype(low)
    expanded = dot(normed_second, expand_w) + expand_bias
    activated = gelu_exact(expanded).astype(low)
    result = middle + pair_sum(dot(activated, reduce_w)) + shifts[-1]
    kept = (stream, normed_first, queries, keys, values, log_total, mixed, middle, normed_second, expanded, activated)
    return result, kept


def column_sum(block):
    return jnp.sum(block.astype(wide), axis=0)


def backward_layer(grad, kept, live, weights, vectors):
    stream, normed_first, queries, keys, values, log_total, mixed, middle, normed_second, expanded, activated = kept
    joint_w, output_w, expand_w, reduce_w = weights
    gains, shifts, joint_bias, expand_bias = vectors
    rows = stream.shape[0]
    grad_low = grad.astype(low)
    grad_reduce = dot(activated.T, grad_low).astype(low)
    grad_act = dot(grad_low, reduce_w.T)
    expanded_low = jax.vjp(gelu_exact, expanded)[1](grad_act)[0].astype(low)
    grad_expand = dot(normed_second.T, expanded_low).astype(low)
    grad_normed = pair_sum(dot(expanded_low, expand_w.T))
    pull_second = jax.vjp(normalize, middle, gains[1], shifts[4])[1]
    grad_norm, grad_gain_two, grad_shift_two = pull_second(grad_normed)
    grad_middle = grad + grad_norm
    middle_low = grad_middle.astype(low)
    grad_output = dot(mixed.T, middle_low).astype(low)
    grad_mixed = dot(middle_low, output_w.T).astype(low).reshape(queries.shape)
    parts = attend_back(queries, keys, values, live, log_total, grad_mixed)
    joint_low = join_heads([part.astype(low).reshape(rows, -1) for part in parts])
    grad_joint = dot(normed_first.T, joint_low).astype(low)
    grad_normed_first = pair_sum(dot(joint_low, joint_w.T))
    pull_first = jax.vjp(normalize, stream, gains[0], shifts[0])[1]
    grad_norm_first, grad_gain_one, grad_shift_one = pull_first(grad_normed_first)
    sums = (
        grad_gain_one,
        grad_gain_two,
        grad_shift_one,
        column_sum(joint_low),
        column_sum(middle_low),
        grad_shift_two,
        column_sum(expanded_low),
        column_sum(grad_low),
    )
    return grad_middle + grad_norm_first, (grad_joint, grad_output, grad_expand, grad_reduce), sums


def adamw_update(weight, gradient, first, second, shrink):
    first_new = beta_one * first + (1.0 - beta_one) * gradient
    second_new = beta_two * second + (1.0 - beta_two) * gradient * gradient
    first_hat = first_new / (1.0 - beta_one**STEP)
    second_hat = second_new / (1.0 - beta_two**STEP)
    delta = -rate * (first_hat / (jnp.sqrt(second_hat) + adam_eps) + shrink * weight)
    return (first_new, second_new, delta)


def gather_vectors(gains, biases):
    block = jnp.concatenate([gains, biases], axis=1).astype(low)
    layers, count, width = block.shape
    block = block.reshape(layers * count, 1, width)
    spread = 1
    for name in ("line", "mid", "pair", "top"):
        for bit in range(bits_of(name)):
            block = double(block, name, bit, spread)
    return block.reshape(layers, count, -1)


def per_device(*args):
    block_input, live_mask, cotangent = args[:3]
    masters = args[3:9]
    momenta = args[9:15]
    variances = args[15:21]
    layer_count = masters[0].shape[0]
    width = block_input.shape[2]
    count, length = block_input.shape[:2]
    tops = lax.axis_size("top")
    here = lax.axis_index("pair")

    lowered = [master.astype(low) for master in masters[:4]]
    vectors_all = gather_vectors(masters[4], masters[5]).astype(wide)
    stream = to_images(block_input).astype(wide)
    live = mask_of_image(live_mask)

    weights = []
    vectors = []
    for layer in range(layer_count):
        joint = gather_block(trade(joint_columns(lowered[0][layer], tops)), 1)
        output = gather_block(lowered[1][layer], 0)
        expand = gather_block(trade(expand_columns(lowered[2][layer], tops)), 1)
        reduce = gather_block(lowered[3][layer], 0)
        weights.append((joint, output, expand, reduce))
        both = vectors_all[layer]
        gains, shifts = both[:2], both[2:]
        bias_view = jnp.stack([shifts[1], jnp.zeros_like(shifts[1]), shifts[2]])
        bias_view = joint_columns(bias_view.reshape(1, -1), tops)
        joint_bias = pick(bias_view, here, 0)[0]
        expand_bias = pick(expand_columns(shifts[5:-1].reshape(1, -1), tops), here, 0)[0]
        vectors.append((gains, shifts, joint_bias, expand_bias))

    saved = []
    for layer in range(layer_count):
        stream, kept = forward_layer(stream, live, weights[layer], vectors[layer])
        saved.append(kept)
    live_float = live.astype(wide)[:, None]
    grad = to_images(cotangent).astype(wide) * live_float
    block_output = from_images((stream * live_float).astype(low), count, length).astype(wide)

    owned = [None] * layer_count
    small = [None] * layer_count
    for layer in reversed(range(layer_count)):
        grad, terms, sums = backward_layer(grad, saved[layer], live, weights[layer], vectors[layer])
        shapes = [master.shape[1] for master in masters[:4]]
        reduce_g = scatter_block(terms[3], 0, shapes[3])
        expand_g = expand_columns_back(trade(scatter_block(terms[2], 1, shapes[2]).reshape(2, shapes[2], -1)), tops)
        output_g = scatter_block(terms[1], 0, shapes[1])
        joint_g = joint_columns_back(trade(scatter_block(terms[0], 1, shapes[0])), tops)
        owned[layer] = [joint_g, output_g, expand_g, reduce_g]
        gain_one, gain_two, shift_one, joint_sum, middle_sum, shift_two, expand_sum, grad_sum = sums
        own_block = width // (2 * tops)
        full = jnp.stack([gain_one, gain_two, shift_one, middle_sum, shift_two, grad_sum])
        full = pick(full.reshape(6, tops, 2, own_block), here, 2)
        mine = joint_sum.reshape(2, 3, tops // 2, own_block)
        query_sum, value_sum = (mine[:, k].reshape(1, tops, own_block) for k in (0, 2))
        expand_all = double(expand_sum.reshape(tops, -1), "pair", 0, 1)
        expand_all = pick(expand_all.reshape(-1, tops, 2, own_block), here, 2)
        small[layer] = jnp.concatenate(
            [full[0:3], query_sum, value_sum, full[3:5], expand_all, full[5:6]], axis=0
        )
    input_grad = from_images(grad.astype(low), count, length).astype(wide)

    block = jnp.concatenate(small, axis=0)
    rows = block.shape[0]
    for name in ("top", "mid", "line"):
        for bit in reversed(range(bits_of(name))):
            block = halve(block.reshape(rows, 2, -1), name, bit, 1, wide)
    block = block.reshape(layer_count, -1, masters[4].shape[2])
    gradients = [jnp.stack([owned[layer][k] for layer in range(layer_count)]) for k in range(4)]
    gradients += [block[:, : masters[4].shape[1]], block[:, masters[4].shape[1] :]]
    firsts, seconds, deltas = [], [], []
    for k in range(6):
        shrink = decay if k < 4 else 0.0
        first_new, second_new, delta = adamw_update(masters[k], gradients[k], momenta[k], variances[k], shrink)
        firsts.append(first_new)
        seconds.append(second_new)
        deltas.append(delta)
    return tuple([block_output, input_grad] + gradients + firsts + seconds + deltas)


def solution(mesh):
    dp, seq = mesh.shape["dp"], mesh.shape["seq"]
    tops = min(4, dp // 2)
    inner = Mesh(mesh.devices.reshape(tops, 2, dp // (2 * tops), seq), ("top", "pair", "mid", "line"))
    rows = ("top", "pair", "mid")
    everyone = rows + ("line",)
    tokens = P(rows, "line", None)
    matrix = P(None, everyone, None)
    vector = P(None, None, everyone)
    params = (matrix,) * 4 + (vector,) * 2
    return jax.shard_map(
        per_device,
        mesh=inner,
        in_specs=(tokens, P(rows, "line"), tokens) + params * 3,
        out_specs=(tokens, tokens) + params * 4,
        check_vma=False,
    )
```
